128 devices in a mesh: cell: 64 (over x, y, z), gpt: 2 (over core).
Axes of the slice: x: 4, y: 4, z: 4, core: 2. Of those that a mesh axis runs over, the one named last changes fastest.
Arguments:
- fields: bfloat16 [6, 16, 524288], P(None, None, 'cell'), may hold values from 0.00099 to 0.1002, as said below
- surface: bfloat16 [2, 524288], P(None, 'cell'), may hold values from 0.19921875 to 0.94921875
- sunlit: int32 [524288], P('cell'), may hold values from 0 to 1
- routing: int32 [4096], P('cell'), may hold values from -1 to 63, as said below
- stencil: int32 [7, 524288], P(None, 'cell'), may hold values from -128 to 128
- weights: float32 [7, 524288], P(None, 'cell'), may hold values from 0.1 to 1
- optics: float32 [3, 112], P(None, 'gpt'), may hold values from 0.05 to 20
- solar_flux: float32 [112], P('gpt'), may hold values from 0.5 to 2
Outputs:
- heating_rate: float32 [16, 524288], P('gpt', 'cell')
The draws below stay inside these ranges and needn't reach their ends.
Inputs may be any that keep to these rules, and one draw needn't show every extreme that they name: `routing`: each device is named by exactly 32 blocks in all, and by at most 1 of the 64 blocks of any one device. All fields are positive.
All inputs are finite; a program needn't handle non-finite values.
Results may differ from the reference program's by a relative error of at most 0.0003.
Values may be sent and summed in bfloat16 or wider, within the bound.
No kernel may reach another device: no remote copies, remote signals or barrier semaphores. Data moves between devices by JAX's collectives and lax.ppermute only.
A program may use at most 64 MiB of HBM per device.

```python
import math
import jax
import jax.numpy as jnp
from jax import lax

G = 112
L = 16
BLK = 128
NB = 64
STEN = 7
HW = 128
NCOL = 524288
N_CELL = 64


def route_plan(key):
    half_cells = N_CELL // 2
    layers = NB // N_CELL
    key_shift, key_moved, key_flip, key_shuffle = jax.random.split(jax.random.fold_in(key, 11), 4)
    shift_value = jax.random.randint(key_shift, (), 0, N_CELL)
    moved = jax.random.randint(key_moved, (layers, half_cells), 0, half_cells + 1).at[:, 0].set(half_cells)
    flipped = jax.random.randint(key_flip, (half_cells,), 0, 2)
    source_ids = jnp.arange(N_CELL, dtype=jnp.int32)[:, None]
    target_ids = jnp.arange(N_CELL, dtype=jnp.int32)[None, :]
    pair_index = source_ids % half_cells
    taker = (source_ids < half_cells) != (flipped[pair_index] == 1)
    partner = (source_ids + half_cells) % N_CELL
    offset_own = (target_ids - source_ids - shift_value) % N_CELL
    offset_partner = (target_ids - partner - shift_value) % N_CELL
    base_plan = offset_own < half_cells
    move_count = moved[:, pair_index[:, 0]][:, :, None]
    losing = jnp.logical_not(taker)[None] & (offset_own[None] < move_count)
    gaining = taker[None] & (offset_partner[None] < move_count)
    assignment = base_plan[None] & jnp.logical_not(losing) | gaining
    counts = jnp.sum(assignment.astype(jnp.int32), axis=0)
    running = jnp.cumsum(counts, axis=1)
    sent_count = running[:, -1]
    position = jnp.arange(NB, dtype=jnp.int32)
    target_of = jnp.sum((running[:, None, :] <= position[None, :, None]).astype(jnp.int32), axis=2)
    assigned = jnp.where(position[None, :] < sent_count[:, None], target_of, -1).astype(jnp.int32)
    shuffles = jax.vmap(lambda each_key: jax.random.permutation(each_key, NB))(jax.random.split(key_shuffle, N_CELL))
    destination = jnp.take_along_axis(assigned, shuffles.astype(jnp.int32), axis=1)
    return destination.reshape(-1).astype(jnp.int32)


def draw_routing(key, part):
    return route_plan(key)


def draw_sunlit(key, part):
    light_draw = jax.random.randint(jax.random.fold_in(key, 13), (NCOL,), 0, 20) < 17
    return light_draw.astype(jnp.int32)


def draw_stencil(key, part):
    offsets = jax.random.randint(jax.random.fold_in(key, 23), (STEN, NCOL), -HW, HW + 1)
    offsets = offsets.at[0, 0].set(-HW)
    offsets = offsets.at[1, 1].set(HW)
    return offsets.astype(jnp.int32)


def draw_fields(key, part):
    lower_ends = jnp.array([0.02, 0.005, 0.002, 0.001, 0.001, 0.001], jnp.float32)[:, None, None]
    upper_ends = jnp.array([0.06, 0.1, 0.02, 0.1, 0.05, 0.01], jnp.float32)[:, None, None]
    uniform_draw = jax.random.uniform(jax.random.fold_in(key, 31), (6, L, NCOL), jnp.float32)
    values = lower_ends * jnp.exp(uniform_draw * jnp.log(upper_ends / lower_ends))
    return values.astype(jnp.bfloat16)


def block_scale(rng, dims, cuts, smallest, largest):
    factor_of = 1.0
    for dim, parts in cuts:
        heights = jax.random.uniform(jax.random.fold_in(jax.random.fold_in(rng, 6), dim), (parts,), jnp.float32, smallest / len(cuts), largest / len(cuts))
        factor_of = factor_of * jnp.repeat(jnp.exp(heights), dims[dim] // parts).reshape((-1,) + (1,) * (len(dims) - 1 - dim))
    return factor_of


def setup_inputs(seed: int = 0) -> dict:
    keys = jax.random.split(jax.random.key(seed), 9)
    fields = draw_fields(jax.random.fold_in(keys[8], 71), 0)
    surface = jnp.clip(0.19921875 + 0.75 * jax.random.uniform(keys[1], (2, NCOL), jnp.float32) ** block_scale(keys[1], (2, NCOL), ((1, 64),), -0.2, 0.2), 0.19921875, 0.94921875).astype(jnp.bfloat16)
    sunlit = draw_sunlit(jax.random.fold_in(keys[8], 71), 0)
    routing = draw_routing(jax.random.fold_in(keys[8], 71), 0)
    stencil = draw_stencil(jax.random.fold_in(keys[8], 71), 0)
    weights = jnp.clip(0.1 + 0.9 * jax.random.uniform(keys[5], (STEN, NCOL), jnp.float32) ** block_scale(keys[5], (STEN, NCOL), ((1, 64),), -0.2, 0.2), 0.1, 1.0)
    optics = jnp.clip(jnp.exp(math.log(20.0) - 5.9914645 * jax.random.uniform(keys[6], (3, G), jnp.float32) ** block_scale(keys[6], (3, G), ((1, 2),), -0.2, 0.2)), 0.05, 20.0)
    solar_flux = jnp.clip(jnp.exp(math.log(2.0) - 1.3862944 * jax.random.uniform(keys[7], (G,), jnp.float32) ** block_scale(keys[7], (G,), ((0, 2),), -0.2, 0.2)), 0.5, 2.0)
    return dict(fields=fields, surface=surface, sunlit=sunlit, routing=routing, stencil=stencil, weights=weights, optics=optics, solar_flux=solar_flux)


def column_heat(fields, geometry, optics, solar_flux, factor):
    levels = fields.shape[1]
    cosine = geometry[0].astype(jnp.float32)[None, :]
    albedo = geometry[1].astype(jnp.float32)[None, :]
    lit_part = geometry[2].astype(jnp.float32)[None, :]
    k_vapor = optics[0][:, None]
    k_ozone = optics[1][:, None]
    k_rayleigh = optics[2][:, None]
    incoming = solar_flux[:, None] * lit_part * cosine
    optical_depth = jnp.zeros_like(incoming)
    scattering = []
    absorbed = []
    direct = []
    for layer_index in range(levels):
        column = fields[:, layer_index].astype(jnp.float32)
        clouds = column[3] + column[4]
        scatter_now = k_rayleigh * column[0] + 0.9 * clouds + 0.8 * column[5]
        absorb_now = k_vapor * column[1] + k_ozone * column[2] + 0.1 * clouds + 0.2 * column[5]
        optical_depth = optical_depth + scatter_now + absorb_now
        scattering.append(scatter_now)
        absorbed.append(absorb_now)
        direct.append(incoming * jnp.exp(-optical_depth / cosine))
    coupling = [0.5 * (scattering[i] + scattering[i + 1]) + 0.1 for i in range(levels - 1)]
    ratios = []
    partial_sol = []
    for layer_index in range(levels):
        above = coupling[layer_index - 1] if layer_index > 0 else 0.5
        below = coupling[layer_index] if layer_index < levels - 1 else 0.5
        diagonal = absorbed[layer_index] + above + below
        source = scattering[layer_index] * direct[layer_index]
        if layer_index == levels - 1:
            source = source + albedo * direct[layer_index]
        if layer_index > 0:
            pivots = diagonal - above * ratios[layer_index - 1]
            solved = (source + above * partial_sol[layer_index - 1]) / pivots
        else:
            pivots = diagonal
            solved = source / pivots
        ratios.append(below / pivots)
        partial_sol.append(solved)
    diffuse = partial_sol[levels - 1]
    heat_rows = [None] * levels
    for layer_index in reversed(range(levels)):
        if layer_index < levels - 1:
            diffuse = partial_sol[layer_index] + ratios[layer_index] * diffuse
        heat_rows[layer_index] = jnp.sum(absorbed[layer_index] * (diffuse + direct[layer_index]), axis=0) * factor
    return jnp.stack(heat_rows)


def reference(fields, surface, sunlit, routing, stencil, weights, optics, solar_flux):
    column_total = fields.shape[2]
    block_total = column_total // BLK
    routed = jnp.repeat((routing >= 0).astype(jnp.float32), BLK)
    geometry = jnp.stack([surface[0].astype(jnp.float32), surface[1].astype(jnp.float32), sunlit.astype(jnp.float32) * routed])
    field_blocks = jnp.moveaxis(fields.reshape(6, L, block_total, BLK), 2, 0)
    geometry_blocks = jnp.moveaxis(geometry.reshape(3, block_total, BLK), 1, 0)
    factor = 1.0 / G

    def one_block(pieces):
        return column_heat(pieces[0], pieces[1], optics, solar_flux, factor)

    heating = lax.map(one_block, (field_blocks, geometry_blocks))
    heating = jnp.moveaxis(heating, 0, 1).reshape(L, column_total)
    normalized = weights / jnp.sum(weights, axis=0, keepdims=True)
    neighbour = (jnp.arange(column_total, dtype=jnp.int32)[None, :] + stencil) % column_total
    result = jnp.zeros((L, column_total), jnp.float32)
    for stencil_point in range(STEN):
        result = result + normalized[stencil_point][None, :] * heating[:, neighbour[stencil_point]]
    return result
```

```python
import functools
import math

import jax
import jax.numpy as jnp
from jax import lax
from jax.experimental import pallas as pl
from jax.experimental.pallas import tpu as pltpu
from jax.sharding import PartitionSpec as P

G = 112
BLK = 128
LOG2E = 1.4426950408889634
LN2 = 0.6931471805599453


def solve_block(b, fields_ref, surf_ref, rows_ref, coef_ref, ratio_ref, part_ref, absn_ref, dir_ref):
    levels = fields_ref.shape[1]
    sl = pl.ds(pl.multiple_of(b * BLK, BLK), BLK)
    col = [fields_ref[i, :, sl].astype(jnp.float32) for i in range(6)]
    clouds = col[3] + col[4]
    rows_ref[0] = col[0]
    rows_ref[1] = col[1]
    rows_ref[2] = col[2]
    rows_ref[3] = 0.9 * clouds + 0.8 * col[5]
    rows_ref[4] = 0.1 * clouds + 0.2 * col[5]
    surf = surf_ref[:, sl].astype(jnp.float32)
    mu = surf[0:1]
    albedo = surf[1:2]
    slope = -LOG2E / mu
    k_ray = coef_ref[0]
    k_vap = coef_ref[1]
    k_ozo = coef_ref[2]
    depth = coef_ref[3] * (-LN2 * mu)

    def optical(l):
        f = [rows_ref[i, l : l + 1, :] for i in range(5)]
        scat = k_ray * f[0] + f[3]
        absn = k_vap * f[1] + k_ozo * f[2] + f[4]
        return scat, absn

    scat, absn = optical(0)
    ratio = None
    excess = None
    carried = None
    for l in range(levels):
        depth = depth + (scat + absn)
        direct = jnp.exp2(depth * slope)
        absn_ref[l] = absn
        dir_ref[l] = direct
        source = scat * direct
        if l == levels - 1:
            source = source + albedo * direct
        if l == 0:
            excess = absn + 0.5
            carried = source
        else:
            excess = absn + ratio * excess
            carried = source + ratio * carried
        if l < levels - 1:
            scat_next, absn_next = optical(l + 1)
            below = 0.5 * (scat + scat_next) + 0.1
        else:
            below = 0.5
        inverse = 1.0 / (excess + below)
        ratio = below * inverse
        part = carried * inverse
        if l < levels - 1:
            ratio_ref[l] = ratio
            part_ref[l] = part
            scat, absn = scat_next, absn_next
    diffuse = part
    heat = [None] * levels
    for l in reversed(range(levels)):
        if l < levels - 1:
            diffuse = part_ref[l] + ratio_ref[l] * diffuse
        heat[l] = jnp.sum(absn_ref[l] * (diffuse + dir_ref[l]), axis=0, keepdims=True)
    return jnp.concatenate(heat, axis=0), mu


def solve_kernel(route_ref, half_ref, fields_ref, surf_ref, lit_ref, coef_ref,
                 own_ref, send_ref, *scratch):
    half = half_ref[0]
    blocks = route_ref.shape[0]
    rows = own_ref.shape[0]

    def body(b, _):
        sl = pl.ds(pl.multiple_of(b * BLK, BLK), BLK)

        @pl.when(route_ref[b] >= 0)
        def _():
            heat, mu = solve_block(b, fields_ref, surf_ref, scratch[0], coef_ref, *scratch[1:])
            lit = lit_ref[pl.ds(b, 1), :].astype(jnp.float32)
            heat = heat * (lit * mu * (1.0 / G))
            top, low = heat[:rows], heat[rows:]
            first = half == 0
            own_ref[:, sl] = jnp.where(first, top, low)
            send_ref[:, sl] = jnp.where(first, low, top)

        @pl.when(route_ref[b] < 0)
        def _():
            own_ref[:, sl] = jnp.zeros((rows, BLK), jnp.float32)
            send_ref[:, sl] = jnp.zeros((rows, BLK), jnp.float32)

        return 0

    lax.fori_loop(0, blocks, body, 0)


def solve(route, half, fields, surface, lit, coef):
    levels, columns = fields.shape[1], fields.shape[2]
    g = coef.shape[1]
    vm = pl.BlockSpec(memory_space=pltpu.VMEM)
    sm = pl.BlockSpec(memory_space=pltpu.SMEM)
    out = jax.ShapeDtypeStruct((levels // 2, columns), jnp.float32)
    return pl.pallas_call(
        solve_kernel,
        out_shape=(out, out),
        in_specs=[sm, sm, vm, vm, vm, vm],
        out_specs=(vm, vm),
        scratch_shapes=[pltpu.VMEM((5, levels, BLK), jnp.float32)]
        + [pltpu.VMEM((levels, g, BLK), jnp.float32)] * 4,
        name="solve",
    )(route, half, fields, surface, lit, coef)


def interp_kernel(own_ref, recv_ref, lo_ref, lo2_ref, hi_ref, hi2_ref, stencil_ref, weights_ref,
                  out_ref, ext_ref):
    columns = own_ref.shape[1]
    points = stencil_ref.shape[0]
    rows = own_ref.shape[0]
    ext_ref[:, 0:BLK] = lo_ref[...] + lo2_ref[...]
    ext_ref[:, BLK : BLK + columns] = own_ref[...] + recv_ref[...]
    ext_ref[:, BLK + columns :] = hi_ref[...] + hi2_ref[...]
    lane = lax.broadcasted_iota(jnp.int32, (rows, BLK), 1) + BLK

    def body(b, _):
        base = pl.multiple_of(b * BLK, BLK)
        sl = pl.ds(base, BLK)
        window = [ext_ref[:, pl.ds(pl.multiple_of(base + i * BLK, BLK), BLK)] for i in range(3)]
        total = jnp.zeros((rows, BLK), jnp.float32)
        norm = jnp.zeros((1, BLK), jnp.float32)
        for j in range(points):
            place = lane + stencil_ref[j : j + 1, sl]
            index = place & (BLK - 1)
            picked = [jnp.take_along_axis(w, index, axis=1) for w in window]
            value = jnp.where(place < BLK, picked[0], jnp.where(place < 2 * BLK, picked[1], picked[2]))
            weight = weights_ref[j : j + 1, sl]
            total = total + weight * value
            norm = norm + weight
        out_ref[:, sl] = total / norm
        return 0

    lax.fori_loop(0, columns // BLK, body, 0)


def interp(own, recv, lo, lo2, hi, hi2, stencil, weights):
    rows, columns = own.shape
    vm = pl.BlockSpec(memory_space=pltpu.VMEM)
    return pl.pallas_call(
        interp_kernel,
        out_shape=jax.ShapeDtypeStruct((rows, columns), jnp.float32),
        in_specs=[vm] * 8,
        out_specs=vm,
        scratch_shapes=[pltpu.VMEM((rows, columns + 2 * BLK), jnp.float32)],
        name="interp",
    )(own, recv, lo, lo2, hi, hi2, stencil, weights)


def local(fields, surface, sunlit, routing, stencil, weights, optics, solar_flux):
    blocks = routing.shape[0]
    half = lax.axis_index("gpt").astype(jnp.int32).reshape(1)
    coef = jnp.concatenate([optics[2:3], optics[0:1], optics[1:2], jnp.log2(solar_flux)[None]])
    coef = jnp.broadcast_to(coef[:, :, None], coef.shape + (BLK,))
    own, send = solve(routing, half, fields, surface, sunlit.reshape(blocks, BLK), coef)
    cells = lax.axis_size("cell")
    pair = lax.axis_size("gpt")
    flat = [(c, k) for c in range(cells) for k in range(pair)]

    def shift(x, step, flip):
        perm = [
            (c * pair + k, ((c + step) % cells) * pair + (k ^ flip)) for c, k in flat
        ]
        return lax.ppermute(x, ("cell", "gpt"), perm)

    recv = shift(send, 0, 1)
    lo = shift(own[:, -BLK:], 1, 0)
    lo2 = shift(send[:, -BLK:], 1, 1)
    hi = shift(own[:, :BLK], -1, 0)
    hi2 = shift(send[:, :BLK], -1, 1)
    return interp(own, recv, lo, lo2, hi, hi2, stencil, weights)


def solution(mesh):
    placed = (
        P(None, None, "cell"),
        P(None, "cell"),
        P("cell"),
        P("cell"),
        P(None, "cell"),
        P(None, "cell"),
        P(None, "gpt"),
        P("gpt"),
    )
    return jax.shard_map(
        local, mesh=mesh, in_specs=placed, out_specs=P("gpt", "cell"), check_vma=False
    )
```
